32 devices in a mesh: grp: 2 (over y), seq: 8 (over z, x), tp: 2 (over core).
Axes of the slice: x: 2, y: 2, z: 4, core: 2. Of those that a mesh axis runs over, the one named last changes fastest.
Arguments:
- hidden: bfloat16 [8, 8192], P('grp', 'seq'), parts along dimension 0, may hold values from -40 to 40
- norm_gain: float32 [8192], P('seq'), may hold values from 0.25 to 1.75
- query_proj: bfloat16 [8192, 4096], P('seq', 'tp'), may hold values from -0.0625 to 0.0625
- keyval_proj: bfloat16 [8192, 2, 512], P('seq', None, 'tp'), may hold values from -0.0625 to 0.0625
- attend_proj: bfloat16 [4096, 8192], P('tp', 'seq'), may hold values from -0.09375 to 0.09375
- keyval_cache: bfloat16 [2, 8, 512, 512], P(None, 'grp', 'seq', 'tp'), parts along dimension 1, may hold values from -320 to 320
- lengths: int32 [8], P('grp'), parts along dimension 0, may hold values from 1 to 512, as said below
Outputs:
- hidden_out: bfloat16 [8, 8192], P('grp', 'seq'), parts along dimension 0
- new_keyval: bfloat16 [8, 2, 512], P('grp', None, 'tp'), parts along dimension 0
The draws below stay inside these ranges and needn't reach their ends.
There are 2 independent parts, one for each index of `grp`. The reference program is written for one: setup_inputs(seed, part) draws one part's arguments, and reference() takes and returns one part's arrays. A program takes and returns all parts, laid end to end along the dimension named above; an argument that names none is the same for every part. Nothing has to cross between parts.
Inputs may be any that keep to these rules, and one draw needn't show every extreme that they name: `lengths`: live cached positions of each request; in every draw some request has all 512.
All inputs are finite; a program needn't handle non-finite values.
Results may differ from the reference program's by a relative error of at most 0.0087.
Values sent between devices are 32-bit elements; how exact they have to be, the bound alone decides.
No kernel may reach another device: no remote copies, remote signals or barrier semaphores. Data moves between devices by JAX's collectives and lax.ppermute only.
A program may use at most 64 MiB of HBM per device.

```python
import jax
import jax.numpy as jnp
from jax import lax

D = 8192
QHEADS = 32
KVHEADS = 4
HEAD_DIM = 128
ROWS = 4
CTX_DEV = 64
CTX = 512
N_SEQ = 8


def draw_hidden(key, part):
    noise_key, row_key = jax.random.split(jax.random.fold_in(key, 11), 2)
    columns = jnp.arange(D, dtype=jnp.float32) / D
    row_factor = 10.0 ** jax.random.uniform(row_key, (ROWS, 1), jnp.float32, -0.5, 0.5)
    noise = jnp.clip(jax.random.normal(noise_key, (ROWS, D), jnp.float32), -4.0, 4.0)
    column_factor = 10.0 ** (0.5 * columns - 0.25)
    return jnp.clip(noise * row_factor * column_factor[None, :], -40.0, 40.0).astype(jnp.bfloat16)


def draw_keyval_cache(key, part):
    noise_key = jax.random.fold_in(jax.random.fold_in(key, 23), 0)
    noise = jnp.clip(jax.random.normal(noise_key, (2, ROWS, CTX, KVHEADS * HEAD_DIM), jnp.float32), -5.0, 5.0)
    return jnp.clip(noise, -320.0, 320.0).astype(jnp.bfloat16)


def draw_lengths(key, part):
    length_key, row_key = jax.random.split(jax.random.fold_in(key, 37))
    drawn = jax.random.randint(length_key, (ROWS,), 1, CTX + 1)
    longest = jax.random.randint(row_key, (), 0, ROWS)
    return jnp.where(jnp.arange(ROWS) == longest, CTX, drawn).astype(jnp.int32)


def levels(stream_key, shape, cuts, least, high):
    level, own = 1.0, jax.random.fold_in(stream_key, 6)
    for position, blocks in cuts:
        steps = jnp.exp(jax.random.uniform(jax.random.fold_in(own, position), (blocks,), jnp.float32, least / len(cuts), high / len(cuts)))
        level = level * jnp.repeat(steps, shape[position] // blocks).reshape([-1 if axis == position else 1 for axis in range(len(shape))])
    return level


def gaussian(rng, dims, scale, limit, shards=(), held_as=jnp.bfloat16):
    values = jax.random.normal(rng, dims, jnp.float32) * scale
    if len(shards) > 0:
        values = levels(rng, dims, shards, -0.22, 0.18) * values
    return jnp.clip(values, min=-limit, max=limit).astype(held_as)


def setup_inputs(seed: int = 0, part: int = 0) -> dict:
    key_list = jax.random.split(jax.random.key(seed), 8)
    part_splits = jax.random.split(jax.random.fold_in(key_list[7], part), 8)
    return {
        "hidden": draw_hidden(jax.random.fold_in(jax.random.fold_in(key_list[7], part), 71), part),
        "norm_gain": jnp.clip(1.0 + 0.15 * jax.random.normal(key_list[1], (D,), jnp.float32), 0.25, 1.75),
        "query_proj": gaussian(key_list[2], (D, QHEADS * HEAD_DIM), D ** -0.5, 0.0625, ((0, 8), (1, 2))),
        "keyval_proj": gaussian(key_list[3], (D, 2, KVHEADS * HEAD_DIM), D ** -0.5, 0.0625, ((0, 8), (2, 2))),
        "attend_proj": gaussian(key_list[4], (QHEADS * HEAD_DIM, D), (QHEADS * HEAD_DIM) ** -0.5, 0.09375, ((0, 2), (1, 8))),
        "keyval_cache": draw_keyval_cache(jax.random.fold_in(jax.random.fold_in(key_list[7], part), 71), part),
        "lengths": draw_lengths(jax.random.fold_in(jax.random.fold_in(key_list[7], part), 71), part),
    }


EPSILON = 1e-05
MASKED = -1e+30

def reference(hidden, norm_gain, query_proj, keyval_proj, attend_proj, keyval_cache, lengths):
    row_count = hidden.shape[0]
    one_float = hidden.astype(jnp.float32)
    scale_two = lax.rsqrt(lax.optimization_barrier(jnp.mean(one_float * one_float, axis=1)) + EPSILON)[:, None]
    scaled = (one_float * norm_gain).astype(jnp.bfloat16)
    query = (jnp.dot(scaled, query_proj, preferred_element_type=jnp.float32) * scale_two).astype(jnp.bfloat16)
    new_keyval = (jnp.dot(scaled, keyval_proj.reshape(D, 2 * KVHEADS * HEAD_DIM), preferred_element_type=jnp.float32).reshape(row_count, 2, KVHEADS * HEAD_DIM) * scale_two[:, :, None]).astype(jnp.bfloat16)
    group_share = QHEADS // KVHEADS
    score_scale = HEAD_DIM ** (-0.5)
    query_heads = query.reshape(row_count, KVHEADS, group_share, HEAD_DIM).astype(jnp.float32)
    cache_keys = keyval_cache[0].reshape(row_count, N_SEQ, CTX_DEV, KVHEADS, HEAD_DIM).astype(jnp.float32)
    cache_values = keyval_cache[1].reshape(row_count, N_SEQ, CTX_DEV, KVHEADS, HEAD_DIM).astype(jnp.float32)
    scores = jnp.einsum('rkgd,rbskd->rbkgs', query_heads, cache_keys, precision=lax.Precision.HIGHEST) * score_scale
    positions = jnp.arange(CTX, dtype=jnp.int32).reshape(N_SEQ, CTX_DEV)
    live_mask = (positions[None] < lengths[:, None, None])[:, :, None, None, :]
    scores = jnp.where(live_mask, scores, MASKED)
    block_max = lax.optimization_barrier(jnp.max(scores, axis=4))
    weights = jnp.where(live_mask, jnp.exp(scores - block_max[..., None]), 0.0).astype(jnp.bfloat16)
    weights = lax.optimization_barrier(weights).astype(jnp.float32)
    block_total = lax.optimization_barrier(jnp.sum(weights, axis=4))
    block_out = jnp.einsum('rbkgs,rbskd->rbkgd', weights, cache_values, precision=lax.Precision.HIGHEST)
    best_score = lax.optimization_barrier(jnp.max(block_max, axis=1))
    factor = jnp.exp(block_max - best_score[:, None])
    total_weight = lax.optimization_barrier(jnp.sum(factor * block_total, axis=1))
    gathered = lax.optimization_barrier(jnp.sum(factor[..., None] * block_out, axis=1))
    own_key = new_keyval[:, 0].reshape(row_count, KVHEADS, HEAD_DIM).astype(jnp.float32)
    own_value = new_keyval[:, 1].reshape(row_count, KVHEADS, HEAD_DIM).astype(jnp.float32)
    own_score = jnp.einsum('rkgd,rkd->rkg', query_heads, own_key, precision=lax.Precision.HIGHEST) * score_scale
    top_score = jnp.maximum(best_score, own_score)
    old_weight = jnp.exp(best_score - top_score)
    fresh_weight = jnp.exp(own_score - top_score)
    attended = (old_weight[..., None] * gathered + fresh_weight[..., None] * own_value[:, :, None, :]) / (old_weight * total_weight + fresh_weight)[..., None]
    attended = attended.reshape(row_count, QHEADS * HEAD_DIM).astype(jnp.bfloat16)
    hidden_out = (one_float + jnp.dot(attended, attend_proj, preferred_element_type=jnp.float32)).astype(jnp.bfloat16)
    return (hidden_out, new_keyval)
```

```python
import jax
import jax.numpy as jnp
from jax import lax
from jax.sharding import PartitionSpec as P

D = 8192
HEAD_DIM = 128


EPSILON = 1e-05
MASKED = -1e30


def stages(size):
    bits = size.bit_length() - 1
    out = []
    bit = 0
    if bits % 2:
        out.append((1,))
        bit = 1
    while bit < bits:
        out.append((2 << bit, 3 << bit, 1 << bit))
        bit += 2
    return out


def partners(value, axis, size, offsets):
    return [lax.ppermute(value, axis, [(i, i ^ o) for i in range(size)]) for o in offsets]


def on_device(seq, tp, hidden, norm_gain, query_proj, keyval_proj, attend_proj, keyval_cache, lengths):
    row_count = hidden.shape[0]
    feature_dev = hidden.shape[1]
    seq_rank = lax.axis_index("seq")
    ctx_dev = keyval_cache.shape[2]
    kv_width = keyval_cache.shape[3]
    kv_heads = kv_width // HEAD_DIM
    q_width = query_proj.shape[1]
    q_heads = q_width // HEAD_DIM
    group_share = q_heads // kv_heads
    score_scale = HEAD_DIM ** (-0.5)
    one_float = hidden.astype(jnp.float32)
    scaled = (one_float * norm_gain).astype(jnp.bfloat16)
    squares = jnp.sum(one_float * one_float, axis=1)
    query_part = jnp.dot(scaled, query_proj, preferred_element_type=jnp.float32)
    first = jnp.concatenate(
        [query_part, jnp.broadcast_to(squares[:, None], (row_count, 128))], axis=1
    )
    for offsets in stages(seq):
        others = partners(first, "seq", seq, offsets)
        for other in others:
            first = first + other
    keyval_part = jnp.dot(
        scaled, keyval_proj.reshape(feature_dev, 2 * kv_width), preferred_element_type=jnp.float32
    )
    scale_two = lax.rsqrt(first[:, q_width : q_width + 1] / D + EPSILON)
    query = (first[:, :q_width] * scale_two).astype(jnp.bfloat16)
    query_heads = query.reshape(row_count, kv_heads, group_share, HEAD_DIM)
    cache_keys = keyval_cache[0].reshape(row_count, ctx_dev, kv_heads, HEAD_DIM)
    cache_values = keyval_cache[1].reshape(row_count, ctx_dev, kv_heads, HEAD_DIM)
    scores = (
        jnp.einsum("rkgd,rskd->rkgs", query_heads, cache_keys, preferred_element_type=jnp.float32)
        * score_scale
    )
    positions = seq_rank * ctx_dev + jnp.arange(ctx_dev, dtype=jnp.int32)
    live_mask = (positions[None, :] < lengths[:, None])[:, None, None, :]
    scores = jnp.where(live_mask, scores, MASKED)
    best = jnp.max(scores, axis=3, keepdims=True)
    weights = jnp.where(live_mask, jnp.exp(scores - best), 0.0).astype(jnp.bfloat16)
    total = jnp.sum(lax.optimization_barrier(weights).astype(jnp.float32), axis=3, keepdims=True)
    gathered = jnp.einsum(
        "rkgs,rskd->rkgd", weights, cache_values, preferred_element_type=jnp.float32
    )
    half = HEAD_DIM // 2
    lanes = best.shape[:3] + (half,)
    keyval_sum = keyval_part.reshape(-1, 2 * HEAD_DIM)
    for offsets in stages(seq):
        packed = jnp.concatenate(
            [
                gathered,
                jnp.broadcast_to(best, lanes),
                jnp.broadcast_to(total, lanes),
            ],
            axis=3,
        ).reshape(row_count * q_heads, 2 * HEAD_DIM)
        packed = jnp.concatenate([packed, keyval_sum], axis=0)
        others = partners(packed, "seq", seq, offsets)
        split = row_count * q_heads
        parts = [(gathered, best, total)]
        for other in others:
            att = other[:split].reshape(row_count, kv_heads, group_share, 2 * HEAD_DIM)
            parts.append(
                (
                    att[..., :HEAD_DIM],
                    att[..., HEAD_DIM : HEAD_DIM + 1],
                    att[..., HEAD_DIM + half : HEAD_DIM + half + 1],
                )
            )
            keyval_sum = keyval_sum + other[split:]
        best = parts[0][1]
        for part in parts[1:]:
            best = jnp.maximum(best, part[1])
        factors = [jnp.exp(part[1] - best) for part in parts]
        gathered = sum(f * part[0] for f, part in zip(factors, parts))
        total = sum(f * part[2] for f, part in zip(factors, parts))
    keyval_all = keyval_sum.reshape(row_count, 2, kv_width)
    new_keyval = (keyval_all * scale_two[:, :, None]).astype(jnp.bfloat16)
    own_key = new_keyval[:, 0].reshape(row_count, kv_heads, HEAD_DIM)
    own_value = new_keyval[:, 1].reshape(row_count, kv_heads, HEAD_DIM).astype(jnp.float32)
    own_score = (
        jnp.einsum("rkgd,rkd->rkg", query_heads, own_key, preferred_element_type=jnp.float32)
        * score_scale
    )[..., None]
    top_score = jnp.maximum(best, own_score)
    old_weight = jnp.exp(best - top_score)
    fresh_weight = jnp.exp(own_score - top_score)
    attended = (old_weight * gathered + fresh_weight * own_value[:, :, None, :]) / (
        old_weight * total + fresh_weight
    )
    attended = attended.reshape(row_count, q_width).astype(jnp.bfloat16)
    attend_term = jnp.dot(attended, attend_proj, preferred_element_type=jnp.float32)
    for offsets in stages(tp):
        for other in partners(attend_term, "tp", tp, offsets):
            attend_term = attend_term + other
    hidden_out = (one_float + attend_term).astype(jnp.bfloat16)
    return (hidden_out, new_keyval)


def solution(mesh):
    in_specs = (
        P("grp", "seq"),
        P("seq"),
        P("seq", "tp"),
        P("seq", None, "tp"),
        P("tp", "seq"),
        P(None, "grp", "seq", "tp"),
        P("grp"),
    )
    out_specs = (P("grp", "seq"), P("grp", None, "tp"))

    def body(*args):
        return on_device(mesh.shape["seq"], mesh.shape["tp"], *args)

    return jax.shard_map(
        body, mesh=mesh, in_specs=in_specs, out_specs=out_specs, check_vma=False
    )
```

```python
import functools

import jax
import jax.numpy as jnp
from jax import lax
from jax.experimental import pallas as pl
from jax.experimental.pallas import tpu as pltpu
from jax.sharding import PartitionSpec as P


HEAD_DIM = 128

EPSILON = 1e-05
MASKED = -1e30


COVER = 16 << 20
COVER_OPS = 1 << 30

VMEM = pl.BlockSpec(memory_space=pltpu.VMEM)
SMEM = pl.BlockSpec(memory_space=pltpu.SMEM)


def call(kernel, outs, ins, flops, bytes_accessed, other_ops=0):
    return pl.pallas_call(
        kernel,
        out_shape=outs,
        in_specs=[SMEM if a.dtype == jnp.int32 else VMEM for a in ins],
        out_specs=[VMEM] * len(outs),
        compiler_params=pltpu.CompilerParams(vmem_limit_bytes=16 << 20),
        cost_estimate=pl.CostEstimate(
            flops=flops, bytes_accessed=bytes_accessed, transcendentals=other_ops
        ),
    )(*ins)


def stages(size):
    bits = size.bit_length() - 1
    out = []
    bit = 1
    while bit < bits:
        if bit + 1 < bits:
            out.append((2 << bit, 3 << bit, 1 << bit))
            bit += 2
        else:
            out.append((1 << bit,))
            bit += 1
    return out


def partners(value, axis, size, offsets):
    got = []
    for offset in offsets:
        got.append(lax.ppermute(value, axis, [(i, i ^ offset) for i in range(size)]))
    return got


def widen_kernel(cache_ref, out_ref):
    out_ref[...] = cache_ref[...].astype(jnp.float32)


def query_kernel(hidden_ref, gain_ref, proj_ref, out_ref):
    width = proj_ref.shape[1]
    one_float = hidden_ref[...].astype(jnp.float32)
    scaled = (one_float * gain_ref[...]).astype(jnp.bfloat16)
    squares = jnp.sum(one_float * one_float, axis=1, keepdims=True)
    out_ref[:, width:] = jnp.broadcast_to(squares, (out_ref.shape[0], HEAD_DIM))
    out_ref[:, :width] = jnp.dot(scaled, proj_ref[...], preferred_element_type=jnp.float32)


def attend_kernel(
    features, width, lengths_ref, mine_ref, other_ref, near_ref, far_ref,
    packed_ref, query_ref, scale_ref,
):
    rows = mine_ref.shape[0]
    heads = width // HEAD_DIM
    ctx = near_ref.shape[2]
    kv_heads = near_ref.shape[3] // HEAD_DIM
    share = heads // kv_heads * rows
    split = heads * rows
    scale = lax.rsqrt(
        (mine_ref[:, width : width + HEAD_DIM] + other_ref[:, width : width + HEAD_DIM])
        / features
        + EPSILON
    )
    scale_ref[...] = scale
    query = jnp.concatenate(
        [
            (mine_ref[:, c : c + HEAD_DIM] + other_ref[:, c : c + HEAD_DIM]) * scale
            for c in range(0, width, HEAD_DIM)
        ],
        axis=0,
    ).astype(jnp.bfloat16)
    query_ref[...] = query
    request = lax.broadcasted_iota(jnp.int32, (split, 2 * ctx), 0) % rows
    lane = lax.broadcasted_iota(jnp.int32, (split, 2 * ctx), 1)
    near = lane < ctx
    length = jnp.zeros((split, 2 * ctx), jnp.int32)
    for r in range(rows):
        length = jnp.where(request == r, lengths_ref[r], length)
    rank = lax.axis_index("seq")
    pair = rank + 1 - 2 * (rank % 2)
    position = jnp.where(near, rank * ctx + lane, pair * ctx + lane - ctx)
    live = position < length

    def blocks(kind, k):
        cut = slice(k * HEAD_DIM, (k + 1) * HEAD_DIM)
        return jnp.concatenate(
            [
                ref[kind, r, :, cut].astype(jnp.bfloat16)
                for r in range(rows)
                for ref in (near_ref, far_ref)
            ],
            axis=0,
        )

    scores = []
    for k in range(kv_heads):
        all_scores = lax.dot_general(
            query[k * share : (k + 1) * share],
            blocks(0, k),
            (((1,), (1,)), ((), ())),
            preferred_element_type=jnp.float32,
        )
        own = all_scores[:, : 2 * ctx]
        for r in range(1, rows):
            own = jnp.where(
                request[:share] == r, all_scores[:, 2 * ctx * r : 2 * ctx * (r + 1)], own
            )
        scores.append(own)
    scores = jnp.concatenate(scores, axis=0) * (HEAD_DIM ** (-0.5))
    best = [
        jnp.max(jnp.where(live & side, scores, MASKED), axis=1, keepdims=True)
        for side in (near, ~near)
    ]
    weights = jnp.where(live, jnp.exp(scores - jnp.where(near, best[0], best[1])), 0.0)
    weights = weights.astype(jnp.bfloat16).astype(jnp.float32)
    sides = [jnp.where(side, weights, 0.0) for side in (near, ~near)]
    top = jnp.maximum(best[0], best[1])
    factors = [jnp.exp(b - top) for b in best]
    total = sum(f * jnp.sum(s, axis=1, keepdims=True) for f, s in zip(factors, sides))
    for k in range(kv_heads):
        cut = slice(k * share, (k + 1) * share)
        spread = jnp.concatenate(
            [
                jnp.concatenate(
                    [jnp.where(request[cut] == r, s[cut], 0.0) for r in range(rows)], axis=1
                )
                for s in sides
            ],
            axis=0,
        ).astype(jnp.bfloat16)
        outs = jnp.dot(spread, blocks(1, k), preferred_element_type=jnp.float32)
        packed_ref[cut, :] = factors[0][cut] * outs[:share] + factors[1][cut] * outs[share:]
    column = lax.broadcasted_iota(jnp.int32, (split, HEAD_DIM), 1)
    pair = jnp.where(column == 0, top, jnp.where(column == 1, total, 0.0))
    pair = jnp.concatenate([pair, jnp.zeros((HEAD_DIM - split, HEAD_DIM), jnp.float32)], axis=0)
    packed_ref[split : split + 8, :] = jnp.transpose(pair)[:8]
    for j in range(2 * kv_heads):
        at = width + HEAD_DIM + j * HEAD_DIM
        packed_ref[split + 8 + rows * j : split + 8 + rows * (j + 1), :] = (
            mine_ref[:, at : at + HEAD_DIM] + other_ref[:, at : at + HEAD_DIM]
        )


def unpack(packed, split):
    pair = jnp.transpose(packed[split : split + 8])
    return packed[:split], pair[:split, 0:1], pair[:split, 1:2], packed[split + 8 :]


def merge(parts):
    best = functools.reduce(jnp.maximum, [p[1] for p in parts])
    factors = [jnp.exp(p[1] - best) for p in parts]
    gathered = sum(f * p[0] for f, p in zip(factors, parts))
    total = sum(f * p[2] for f, p in zip(factors, parts))
    return gathered, best, total, sum(p[3] for p in parts)


def merge_kernel(split, *refs):
    gathered, best, total, keyval = merge([unpack(ref[...], split) for ref in refs[:-1]])
    packed_ref = refs[-1]
    packed_ref[:split, :] = gathered
    column = lax.broadcasted_iota(jnp.int32, (split, HEAD_DIM), 1)
    pair = jnp.where(column == 0, best, jnp.where(column == 1, total, 0.0))
    pair = jnp.concatenate([pair, jnp.zeros((HEAD_DIM - split, HEAD_DIM), jnp.float32)], axis=0)
    packed_ref[split : split + 8, :] = jnp.transpose(pair)[:8]
    packed_ref[split + 8 :, :] = keyval


def output_kernel(parts, query_ref, scale_ref, proj_ref, *refs):
    packed, (out_ref, new_ref) = refs[:parts], refs[parts:]
    split = query_ref.shape[0]
    rows = scale_ref.shape[0]
    gathered, best, total, keyval = merge([unpack(ref[...], split) for ref in packed])
    kv_heads = keyval.shape[0] // rows // 2
    group = split // rows // kv_heads
    new = (keyval * jnp.concatenate([scale_ref[...]] * (2 * kv_heads), axis=0)).astype(jnp.bfloat16)
    new = new.astype(jnp.float32)
    for j in range(2 * kv_heads):
        new_ref[:, j * HEAD_DIM : (j + 1) * HEAD_DIM] = new[j * rows : (j + 1) * rows]
    own_key, own_value = (
        jnp.concatenate(
            [
                new[(kind * kv_heads + k) * rows : (kind * kv_heads + k + 1) * rows]
                for k in range(kv_heads)
                for _ in range(group)
            ],
            axis=0,
        )
        for kind in range(2)
    )
    query = query_ref[...].astype(jnp.float32)
    own_score = jnp.sum(query * own_key, axis=1, keepdims=True) * (HEAD_DIM ** (-0.5))
    top = jnp.maximum(best, own_score)
    old_weight = jnp.exp(best - top)
    fresh_weight = jnp.exp(own_score - top)
    attended = (old_weight * gathered + fresh_weight * own_value) / (
        old_weight * total + fresh_weight
    )
    attended = jnp.concatenate(
        [attended[r : r + rows] for r in range(0, split, rows)], axis=1
    ).astype(jnp.bfloat16)
    out_ref[...] = jnp.dot(attended, proj_ref[...], preferred_element_type=jnp.float32)


def on_device(
    seq, tp, hidden, norm_gain, query_proj, keyval_proj, attend_proj, keyval_cache, lengths
):
    f32 = jnp.float32
    rows, feature_dev = hidden.shape
    kv_width = keyval_cache.shape[3]
    width = query_proj.shape[1]
    split = rows * width // HEAD_DIM
    one_float = hidden.astype(f32)

    near = call(
        widen_kernel,
        [jax.ShapeDtypeStruct(keyval_cache.shape, f32)],
        [keyval_cache],
        0,
        COVER,
        COVER_OPS,
    )[0]
    far = partners(near, "seq", seq, (1,))[0]

    first = call(
        query_kernel,
        [jax.ShapeDtypeStruct((rows, width + HEAD_DIM), f32)],
        [hidden, norm_gain.reshape(1, feature_dev), query_proj],
        2 * rows * feature_dev * width,
        COVER,
    )[0]
    for offsets in stages(seq):
        for other in partners(first, "seq", seq, offsets):
            first = first + other
    scaled = (one_float * norm_gain).astype(jnp.bfloat16)
    keyval_part = jnp.dot(
        scaled, keyval_proj.reshape(feature_dev, 2 * kv_width), preferred_element_type=f32
    )
    first = jnp.concatenate([first, keyval_part], axis=1)
    second = partners(first, "seq", seq, (1,))[0]

    pack = jax.ShapeDtypeStruct((split + 8 + rows * 2 * kv_width // HEAD_DIM, HEAD_DIM), f32)
    packed, query, scale = call(
        functools.partial(attend_kernel, float(seq * feature_dev), width),
        [
            pack,
            jax.ShapeDtypeStruct((split, HEAD_DIM), jnp.bfloat16),
            jax.ShapeDtypeStruct((rows, HEAD_DIM), f32),
        ],
        [lengths, first, second, near, far],
        16 * split * keyval_cache.shape[2] * HEAD_DIM,
        COVER,
    )
    todo = stages(seq)
    for place, offsets in enumerate(todo):
        parts = [packed] + partners(packed, "seq", seq, offsets)
        if place < len(todo) - 1:
            packed = call(functools.partial(merge_kernel, split), [pack], parts, 0, COVER)[0]
    term, new_keyval = call(
        functools.partial(output_kernel, len(parts)),
        [
            jax.ShapeDtypeStruct((rows, attend_proj.shape[1]), f32),
            jax.ShapeDtypeStruct((rows, 2 * kv_width), f32),
        ],
        [query, scale, attend_proj, *parts],
        2 * rows * width * attend_proj.shape[1],
        COVER,
    )
    for bit in range(tp.bit_length() - 1):
        term = term + partners(term, "tp", tp, (1 << bit,))[0]
    hidden_out = (one_float + term).astype(jnp.bfloat16)
    return (hidden_out, new_keyval.astype(jnp.bfloat16).reshape(rows, 2, kv_width))


def solution(mesh):
    in_specs = (
        P("grp", "seq"),
        P("seq"),
        P("seq", "tp"),
        P("seq", None, "tp"),
        P("tp", "seq"),
        P(None, "grp", "seq", "tp"),
        P("grp"),
    )
    out_specs = (P("grp", "seq"), P("grp", None, "tp"))

    def body(*args):
        return on_device(mesh.shape["seq"], mesh.shape["tp"], *args)

    return jax.shard_map(
        body, mesh=mesh, in_specs=in_specs, out_specs=out_specs, check_vma=False
    )
```

```python
import functools

import jax
import jax.numpy as jnp
from jax import lax
from jax.experimental import pallas as pl
from jax.experimental.pallas import tpu as pltpu
from jax.sharding import PartitionSpec as P


HEAD_DIM = 128

EPSILON = 1e-05
MASKED = -1e30


COVER = 16 << 20
COVER_OPS = 1 << 22

ORDERS = (
    lambda low, high: (high, low | high, low),
    lambda low, high: (low | high, high, low),
)

VMEM = pl.BlockSpec(memory_space=pltpu.VMEM)
SMEM = pl.BlockSpec(memory_space=pltpu.SMEM)


def call(kernel, outs, ins, flops, bytes_accessed, other_ops=0):
    return pl.pallas_call(
        kernel,
        out_shape=outs,
        in_specs=[SMEM if a.dtype == jnp.int32 else VMEM for a in ins],
        out_specs=[VMEM] * len(outs),
        compiler_params=pltpu.CompilerParams(vmem_limit_bytes=16 << 20),
        cost_estimate=pl.CostEstimate(
            flops=flops, bytes_accessed=bytes_accessed, transcendentals=other_ops
        ),
    )(*ins)


def pair_bit(seq, core):
    return core % min(2, seq.bit_length() - 1)


def stages(seq, core):
    bits = [1 << b for b in range(seq.bit_length() - 1) if b != pair_bit(seq, core)]
    out = []
    while len(bits) > 1:
        low, high, *bits = bits
        out.append(ORDERS[core % 2](low, high))
    return out + [(bit,) for bit in bits]


def exchange(value, seq, tp, offsets):
    got = []
    for pair in zip(*offsets):
        moves = [
            (i * tp + core, (i ^ pair[core]) * tp + core) for i in range(seq) for core in range(tp)
        ]
        got.append(lax.ppermute(value, ("seq", "tp"), moves))
    return got


def widen_kernel(cache_ref, out_ref):
    out_ref[...] = cache_ref[...].astype(jnp.float32)


def query_kernel(hidden_ref, gain_ref, proj_ref, out_ref):
    width = proj_ref.shape[1]
    one_float = hidden_ref[...].astype(jnp.float32)
    scaled = (one_float * gain_ref[...]).astype(jnp.bfloat16)
    squares = jnp.sum(one_float * one_float, axis=1, keepdims=True)
    out_ref[:, width:] = jnp.broadcast_to(squares, (out_ref.shape[0], HEAD_DIM))
    out_ref[:, :width] = jnp.dot(scaled, proj_ref[...], preferred_element_type=jnp.float32)


def blocks_kernel(pair_offset, lengths_ref, near_ref, far_ref, keys_ref, values_ref, live_ref):
    rows, ctx = near_ref.shape[1:3]
    shape = live_ref.shape
    request = lax.broadcasted_iota(jnp.int32, shape, 0) % rows
    lane = lax.broadcasted_iota(jnp.int32, shape, 1)
    length = jnp.zeros(shape, jnp.int32)
    for r in range(rows):
        length = jnp.where(request == r, lengths_ref[r], length)
    rank = lax.axis_index("seq")
    pair = rank ^ pair_offset()
    position = jnp.where(lane < ctx, rank * ctx + lane, pair * ctx + lane - ctx)
    live_ref[...] = jnp.where(position < length, 1.0, 0.0)
    for kind, out_ref in enumerate((keys_ref, values_ref)):
        for k in range(out_ref.shape[0]):
            for r in range(rows):
                for side, ref in enumerate((near_ref, far_ref)):
                    at = (2 * r + side) * ctx
                    out_ref[k, at : at + ctx, :] = ref[
                        kind, r, :, k * HEAD_DIM : (k + 1) * HEAD_DIM
                    ].astype(jnp.bfloat16)


def attend_kernel(
    features, width, mine_ref, other_ref, keys_ref, values_ref, live_ref,
    packed_ref, query_ref, scale_ref,
):
    rows = mine_ref.shape[0]
    heads = width // HEAD_DIM
    kv_heads = keys_ref.shape[0]
    ctx = keys_ref.shape[1] // rows // 2
    share = heads // kv_heads * rows
    split = heads * rows
    scale = lax.rsqrt(
        (mine_ref[:, width : width + HEAD_DIM] + other_ref[:, width : width + HEAD_DIM])
        / features
        + EPSILON
    )
    scale_ref[...] = scale
    query = jnp.concatenate(
        [
            (mine_ref[:, c : c + HEAD_DIM] + other_ref[:, c : c + HEAD_DIM]) * scale
            for c in range(0, width, HEAD_DIM)
        ],
        axis=0,
    ).astype(jnp.bfloat16)
    query_ref[...] = query
    request = lax.broadcasted_iota(jnp.int32, (split, 2 * ctx), 0) % rows
    near = lax.broadcasted_iota(jnp.int32, (split, 2 * ctx), 1) < ctx
    live = live_ref[...] > 0
    scores = []
    for k in range(kv_heads):
        all_scores = lax.dot_general(
            query[k * share : (k + 1) * share],
            keys_ref[k],
            (((1,), (1,)), ((), ())),
            preferred_element_type=jnp.float32,
        )
        own = all_scores[:, : 2 * ctx]
        for r in range(1, rows):
            own = jnp.where(
                request[:share] == r, all_scores[:, 2 * ctx * r : 2 * ctx * (r + 1)], own
            )
        scores.append(own)
    scores = jnp.concatenate(scores, axis=0) * (HEAD_DIM ** (-0.5))
    best = [
        jnp.max(jnp.where(live & side, scores, MASKED), axis=1, keepdims=True)
        for side in (near, ~near)
    ]
    weights = jnp.where(live, jnp.exp(scores - jnp.where(near, best[0], best[1])), 0.0)
    weights = weights.astype(jnp.bfloat16).astype(jnp.float32)
    sides = [jnp.where(side, weights, 0.0) for side in (near, ~near)]
    top = jnp.maximum(best[0], best[1])
    factors = [jnp.exp(b - top) for b in best]
    total = sum(f * jnp.sum(s, axis=1, keepdims=True) for f, s in zip(factors, sides))
    for k in range(kv_heads):
        cut = slice(k * share, (k + 1) * share)
        spread = jnp.concatenate(
            [
                jnp.concatenate(
                    [jnp.where(request[cut] == r, s[cut], 0.0) for r in range(rows)], axis=1
                )
                for s in sides
            ],
            axis=0,
        ).astype(jnp.bfloat16)
        outs = jnp.dot(spread, values_ref[k], preferred_element_type=jnp.float32)
        packed_ref[cut, :] = factors[0][cut] * outs[:share] + factors[1][cut] * outs[share:]
    column = lax.broadcasted_iota(jnp.int32, (split, HEAD_DIM), 1)
    pair = jnp.where(column == 0, top, jnp.where(column == 1, total, 0.0))
    pair = jnp.concatenate([pair, jnp.zeros((HEAD_DIM - split, HEAD_DIM), jnp.float32)], axis=0)
    packed_ref[split : split + 8, :] = jnp.transpose(pair)[:8]
    for j in range(2 * kv_heads):
        at = width + HEAD_DIM + j * HEAD_DIM
        packed_ref[split + 8 + rows * j : split + 8 + rows * (j + 1), :] = (
            mine_ref[:, at : at + HEAD_DIM] + other_ref[:, at : at + HEAD_DIM]
        )


def unpack(packed, split):
    pair = jnp.transpose(packed[split : split + 8])
    return packed[:split], pair[:split, 0:1], pair[:split, 1:2], packed[split + 8 :]


def merge(parts):
    best = functools.reduce(jnp.maximum, [p[1] for p in parts])
    factors = [jnp.exp(p[1] - best) for p in parts]
    gathered = sum(f * p[0] for f, p in zip(factors, parts))
    total = sum(f * p[2] for f, p in zip(factors, parts))
    return gathered, best, total, sum(p[3] for p in parts)


def merge_kernel(split, *refs):
    gathered, best, total, keyval = merge([unpack(ref[...], split) for ref in refs[:-1]])
    packed_ref = refs[-1]
    packed_ref[:split, :] = gathered
    column = lax.broadcasted_iota(jnp.int32, (split, HEAD_DIM), 1)
    pair = jnp.where(column == 0, best, jnp.where(column == 1, total, 0.0))
    pair = jnp.concatenate([pair, jnp.zeros((HEAD_DIM - split, HEAD_DIM), jnp.float32)], axis=0)
    packed_ref[split : split + 8, :] = jnp.transpose(pair)[:8]
    packed_ref[split + 8 :, :] = keyval


def output_kernel(parts, query_ref, scale_ref, proj_ref, *refs):
    packed, (out_ref, new_ref) = refs[:parts], refs[parts:]
    split = query_ref.shape[0]
    rows = scale_ref.shape[0]
    gathered, best, total, keyval = merge([unpack(ref[...], split) for ref in packed])
    kv_heads = keyval.shape[0] // rows // 2
    group = split // rows // kv_heads
    new = (keyval * jnp.concatenate([scale_ref[...]] * (2 * kv_heads), axis=0)).astype(jnp.bfloat16)
    new = new.astype(jnp.float32)
    for j in range(2 * kv_heads):
        new_ref[:, j * HEAD_DIM : (j + 1) * HEAD_DIM] = new[j * rows : (j + 1) * rows]
    own_key, own_value = (
        jnp.concatenate(
            [
                new[(kind * kv_heads + k) * rows : (kind * kv_heads + k + 1) * rows]
                for k in range(kv_heads)
                for _ in range(group)
            ],
            axis=0,
        )
        for kind in range(2)
    )
    query = query_ref[...].astype(jnp.float32)
    own_score = jnp.sum(query * own_key, axis=1, keepdims=True) * (HEAD_DIM ** (-0.5))
    top = jnp.maximum(best, own_score)
    old_weight = jnp.exp(best - top)
    fresh_weight = jnp.exp(own_score - top)
    attended = (old_weight * gathered + fresh_weight * own_value) / (
        old_weight * total + fresh_weight
    )
    attended = jnp.concatenate(
        [attended[r : r + rows] for r in range(0, split, rows)], axis=1
    ).astype(jnp.bfloat16)
    out_ref[...] = jnp.dot(attended, proj_ref[...], preferred_element_type=jnp.float32)


def on_device(
    seq, tp, hidden, norm_gain, query_proj, keyval_proj, attend_proj, keyval_cache, lengths
):
    f32 = jnp.float32
    rows, feature_dev = hidden.shape
    kv_width = keyval_cache.shape[3]
    width = query_proj.shape[1]
    split = rows * width // HEAD_DIM
    one_float = hidden.astype(f32)
    pairs = [(1 << pair_bit(seq, core),) for core in range(tp)]
    rounds = list(zip(*(stages(seq, core) for core in range(tp))))

    def pair_offset():
        core = lax.axis_index("tp")
        return sum(jnp.where(core == c, offset, 0) for c, (offset,) in enumerate(pairs))

    near = call(
        widen_kernel,
        [jax.ShapeDtypeStruct(keyval_cache.shape, f32)],
        [keyval_cache],
        0,
        COVER,
        COVER_OPS,
    )[0]
    far = exchange(near, seq, tp, pairs)[0]

    first = call(
        query_kernel,
        [jax.ShapeDtypeStruct((rows, width + HEAD_DIM), f32)],
        [hidden, norm_gain.reshape(1, feature_dev), query_proj],
        2 * rows * feature_dev * width,
        COVER,
    )[0]
    for offsets in rounds:
        for other in exchange(first, seq, tp, offsets):
            first = first + other
    scaled = (one_float * norm_gain).astype(jnp.bfloat16)
    keyval_part = jnp.dot(
        scaled, keyval_proj.reshape(feature_dev, 2 * kv_width), preferred_element_type=f32
    )
    first = jnp.concatenate([first, keyval_part], axis=1)
    second = exchange(first, seq, tp, pairs)[0]

    block = jax.ShapeDtypeStruct(
        (kv_width // HEAD_DIM, 2 * rows * keyval_cache.shape[2], HEAD_DIM), jnp.bfloat16
    )
    keys, values, live = call(
        functools.partial(blocks_kernel, pair_offset),
        [block, block, jax.ShapeDtypeStruct((split, 2 * keyval_cache.shape[2]), f32)],
        [lengths, near, far],
        0,
        4 * near.size,
    )
    pack = jax.ShapeDtypeStruct((split + 8 + rows * 2 * kv_width // HEAD_DIM, HEAD_DIM), f32)
    packed, query, scale = call(
        functools.partial(attend_kernel, float(seq * feature_dev), width),
        [
            pack,
            jax.ShapeDtypeStruct((split, HEAD_DIM), jnp.bfloat16),
            jax.ShapeDtypeStruct((rows, HEAD_DIM), f32),
        ],
        [first, second, keys, values, live],
        16 * split * keyval_cache.shape[2] * HEAD_DIM,
        COVER,
    )
    for place, offsets in enumerate(rounds):
        parts = [packed] + exchange(packed, seq, tp, offsets)
        if place < len(rounds) - 1:
            packed = call(functools.partial(merge_kernel, split), [pack], parts, 0, COVER)[0]
    term, new_keyval = call(
        functools.partial(output_kernel, len(parts)),
        [
            jax.ShapeDtypeStruct((rows, attend_proj.shape[1]), f32),
            jax.ShapeDtypeStruct((rows, 2 * kv_width), f32),
        ],
        [query, scale, attend_proj, *parts],
        2 * rows * width * attend_proj.shape[1],
        COVER,
    )
    for bit in range(tp.bit_length() - 1):
        term = term + lax.ppermute(term, "tp", [(i, i ^ (1 << bit)) for i in range(tp)])
    hidden_out = (one_float + term).astype(jnp.bfloat16)
    return (hidden_out, new_keyval.astype(jnp.bfloat16).reshape(rows, 2, kv_width))


def solution(mesh):
    in_specs = (
        P("grp", "seq"),
        P("seq"),
        P("seq", "tp"),
        P("seq", None, "tp"),
        P("tp", "seq"),
        P(None, "grp", "seq", "tp"),
        P("grp"),
    )
    out_specs = (P("grp", "seq"), P("grp", None, "tp"))

    def body(*args):
        return on_device(mesh.shape["seq"], mesh.shape["tp"], *args)

    return jax.shard_map(
        body, mesh=mesh, in_specs=in_specs, out_specs=out_specs, check_vma=False
    )
```

```python
import functools

import jax
import jax.numpy as jnp
from jax import lax
from jax.experimental import pallas as pl
from jax.experimental.pallas import tpu as pltpu
from jax.sharding import PartitionSpec as P


HEAD_DIM = 128

EPSILON = 1e-05
MASKED = -1e30


COVER = 16 << 20
COVER_OPS = 1 << 22

VMEM = pl.BlockSpec(memory_space=pltpu.VMEM)
SMEM = pl.BlockSpec(memory_space=pltpu.SMEM)


def call(kernel, outs, ins, flops, bytes_accessed, other_ops=0):
    return pl.pallas_call(
        kernel,
        out_shape=outs,
        in_specs=[SMEM if a.dtype == jnp.int32 else VMEM for a in ins],
        out_specs=[VMEM] * len(outs),
        compiler_params=pltpu.CompilerParams(vmem_limit_bytes=16 << 20),
        cost_estimate=pl.CostEstimate(
            flops=flops, bytes_accessed=bytes_accessed, transcendentals=other_ops
        ),
    )(*ins)


def pair_bit(seq, core):
    return core % min(2, seq.bit_length() - 1)


def stages(seq, core):
    bits = [1 << b for b in range(seq.bit_length() - 1) if b != pair_bit(seq, core)]
    out = []
    while len(bits) > 1:
        low, high, *bits = bits
        out.append((low | high, high, low))
    return out + [(bit,) for bit in bits]


def exchange(value, seq, tp, offsets):
    got = []
    for pair in zip(*offsets):
        moves = [
            (i * tp + core, (i ^ pair[core]) * tp + core) for i in range(seq) for core in range(tp)
        ]
        got.append(lax.ppermute(value, ("seq", "tp"), moves))
    return got


def widen_kernel(cache_ref, out_ref):
    out_ref[...] = cache_ref[...].astype(jnp.float32)


def query_kernel(hidden_ref, gain_ref, proj_ref, out_ref):
    width = proj_ref.shape[1]
    one_float = hidden_ref[...].astype(jnp.float32)
    scaled = (one_float * gain_ref[...]).astype(jnp.bfloat16)
    squares = jnp.sum(one_float * one_float, axis=1, keepdims=True)
    out_ref[:, width:] = jnp.broadcast_to(squares, (out_ref.shape[0], HEAD_DIM))
    out_ref[:, :width] = jnp.dot(scaled, proj_ref[...], preferred_element_type=jnp.float32)


def blocks_kernel(pair_offset, lengths_ref, near_ref, far_ref, keys_ref, values_ref, live_ref):
    rows, ctx = near_ref.shape[1:3]
    shape = live_ref.shape
    request = lax.broadcasted_iota(jnp.int32, shape, 0) % rows
    lane = lax.broadcasted_iota(jnp.int32, shape, 1)
    length = jnp.zeros(shape, jnp.int32)
    for r in range(rows):
        length = jnp.where(request == r, lengths_ref[r], length)
    rank = lax.axis_index("seq")
    pair = rank ^ pair_offset()
    position = jnp.where(lane < ctx, rank * ctx + lane, pair * ctx + lane - ctx)
    live_ref[...] = jnp.where(position < length, 1.0, 0.0)
    for kind, out_ref in enumerate((keys_ref, values_ref)):
        for k in range(out_ref.shape[0]):
            for r in range(rows):
                for side, ref in enumerate((near_ref, far_ref)):
                    at = (2 * r + side) * ctx
                    out_ref[k, at : at + ctx, :] = ref[
                        kind, r, :, k * HEAD_DIM : (k + 1) * HEAD_DIM
                    ].astype(jnp.bfloat16)


def attend_kernel(
    features, width, mine_ref, other_ref, keys_ref, values_ref, live_ref,
    packed_ref, query_ref, scale_ref,
):
    rows = mine_ref.shape[0]
    heads = width // HEAD_DIM
    kv_heads = keys_ref.shape[0]
    ctx = keys_ref.shape[1] // rows // 2
    share = heads // kv_heads * rows
    split = heads * rows
    scale = lax.rsqrt(
        (mine_ref[:, width : width + HEAD_DIM] + other_ref[:, width : width + HEAD_DIM])
        / features
        + EPSILON
    )
    scale_ref[...] = scale
    query = jnp.concatenate(
        [
            (mine_ref[:, c : c + HEAD_DIM] + other_ref[:, c : c + HEAD_DIM]) * scale
            for c in range(0, width, HEAD_DIM)
        ],
        axis=0,
    ).astype(jnp.bfloat16)
    query_ref[...] = query
    request = lax.broadcasted_iota(jnp.int32, (split, 2 * ctx), 0) % rows
    near = lax.broadcasted_iota(jnp.int32, (split, 2 * ctx), 1) < ctx
    live = live_ref[...] > 0
    scores = []
    for k in range(kv_heads):
        all_scores = lax.dot_general(
            query[k * share : (k + 1) * share],
            keys_ref[k],
            (((1,), (1,)), ((), ())),
            preferred_element_type=jnp.float32,
        )
        own = all_scores[:, : 2 * ctx]
        for r in range(1, rows):
            own = jnp.where(
                request[:share] == r, all_scores[:, 2 * ctx * r : 2 * ctx * (r + 1)], own
            )
        scores.append(own)
    scores = jnp.concatenate(scores, axis=0) * (HEAD_DIM ** (-0.5))
    best = [
        jnp.max(jnp.where(live & side, scores, MASKED), axis=1, keepdims=True)
        for side in (near, ~near)
    ]
    weights = jnp.where(live, jnp.exp(scores - jnp.where(near, best[0], best[1])), 0.0)
    weights = weights.astype(jnp.bfloat16).astype(jnp.float32)
    sides = [jnp.where(side, weights, 0.0) for side in (near, ~near)]
    top = jnp.maximum(best[0], best[1])
    factors = [jnp.exp(b - top) for b in best]
    total = sum(f * jnp.sum(s, axis=1, keepdims=True) for f, s in zip(factors, sides))
    for k in range(kv_heads):
        cut = slice(k * share, (k + 1) * share)
        spread = jnp.concatenate(
            [
                jnp.concatenate(
                    [jnp.where(request[cut] == r, s[cut], 0.0) for r in range(rows)], axis=1
                )
                for s in sides
            ],
            axis=0,
        ).astype(jnp.bfloat16)
        outs = jnp.dot(spread, values_ref[k], preferred_element_type=jnp.float32)
        packed_ref[cut, :] = factors[0][cut] * outs[:share] + factors[1][cut] * outs[share:]
    column = lax.broadcasted_iota(jnp.int32, (split, HEAD_DIM), 1)
    pair = jnp.where(column == 0, top, jnp.where(column == 1, total, 0.0))
    pair = jnp.concatenate([pair, jnp.zeros((HEAD_DIM - split, HEAD_DIM), jnp.float32)], axis=0)
    packed_ref[split : split + 8, :] = jnp.transpose(pair)[:8]
    for j in range(2 * kv_heads):
        at = width + HEAD_DIM + j * HEAD_DIM
        packed_ref[split + 8 + rows * j : split + 8 + rows * (j + 1), :] = (
            mine_ref[:, at : at + HEAD_DIM] + other_ref[:, at : at + HEAD_DIM]
        )


def unpack(packed, split):
    pair = jnp.transpose(packed[split : split + 8])
    return packed[:split], pair[:split, 0:1], pair[:split, 1:2], packed[split + 8 :]


def merge(parts):
    best = functools.reduce(jnp.maximum, [p[1] for p in parts])
    factors = [jnp.exp(p[1] - best) for p in parts]
    gathered = sum(f * p[0] for f, p in zip(factors, parts))
    total = sum(f * p[2] for f, p in zip(factors, parts))
    return gathered, best, total, sum(p[3] for p in parts)


def merge_kernel(split, *refs):
    gathered, best, total, keyval = merge([unpack(ref[...], split) for ref in refs[:-1]])
    packed_ref = refs[-1]
    packed_ref[:split, :] = gathered
    column = lax.broadcasted_iota(jnp.int32, (split, HEAD_DIM), 1)
    pair = jnp.where(column == 0, best, jnp.where(column == 1, total, 0.0))
    pair = jnp.concatenate([pair, jnp.zeros((HEAD_DIM - split, HEAD_DIM), jnp.float32)], axis=0)
    packed_ref[split : split + 8, :] = jnp.transpose(pair)[:8]
    packed_ref[split + 8 :, :] = keyval


def output_kernel(parts, query_ref, scale_ref, proj_ref, *refs):
    packed, (out_ref, new_ref) = refs[:parts], refs[parts:]
    split = query_ref.shape[0]
    rows = scale_ref.shape[0]
    gathered, best, total, keyval = merge([unpack(ref[...], split) for ref in packed])
    kv_heads = keyval.shape[0] // rows // 2
    group = split // rows // kv_heads
    new = (keyval * jnp.concatenate([scale_ref[...]] * (2 * kv_heads), axis=0)).astype(jnp.bfloat16)
    new = new.astype(jnp.float32)
    for j in range(2 * kv_heads):
        new_ref[:, j * HEAD_DIM : (j + 1) * HEAD_DIM] = new[j * rows : (j + 1) * rows]
    own_key, own_value = (
        jnp.concatenate(
            [
                new[(kind * kv_heads + k) * rows : (kind * kv_heads + k + 1) * rows]
                for k in range(kv_heads)
                for _ in range(group)
            ],
            axis=0,
        )
        for kind in range(2)
    )
    query = query_ref[...].astype(jnp.float32)
    own_score = jnp.sum(query * own_key, axis=1, keepdims=True) * (HEAD_DIM ** (-0.5))
    top = jnp.maximum(best, own_score)
    old_weight = jnp.exp(best - top)
    fresh_weight = jnp.exp(own_score - top)
    attended = (old_weight * gathered + fresh_weight * own_value) / (
        old_weight * total + fresh_weight
    )
    attended = jnp.concatenate(
        [attended[r : r + rows] for r in range(0, split, rows)], axis=1
    ).astype(jnp.bfloat16)
    out_ref[...] = jnp.dot(attended, proj_ref[...], preferred_element_type=jnp.float32)


def on_device(
    seq, tp, hidden, norm_gain, query_proj, keyval_proj, attend_proj, keyval_cache, lengths
):
    f32 = jnp.float32
    rows, feature_dev = hidden.shape
    kv_width = keyval_cache.shape[3]
    width = query_proj.shape[1]
    split = rows * width // HEAD_DIM
    one_float = hidden.astype(f32)
    pairs = [(1 << pair_bit(seq, core),) for core in range(tp)]
    rounds = list(zip(*(stages(seq, core) for core in range(tp))))

    def pair_offset():
        core = lax.axis_index("tp")
        return sum(jnp.where(core == c, offset, 0) for c, (offset,) in enumerate(pairs))

    near = call(widen_kernel, [jax.ShapeDtypeStruct(keyval_cache.shape, f32)], [keyval_cache], 0, COVER, COVER_OPS)[0]
    far = exchange(near, seq, tp, pairs)[0]

    first = call(
        query_kernel,
        [jax.ShapeDtypeStruct((rows, width + HEAD_DIM), f32)],
        [hidden, norm_gain.reshape(1, feature_dev), query_proj],
        2 * rows * feature_dev * width,
        COVER,
    )[0]
    for offsets in rounds:
        for other in exchange(first, seq, tp, offsets):
            first = first + other
    scaled = (one_float * norm_gain).astype(jnp.bfloat16)
    keyval_part = jnp.dot(
        scaled, keyval_proj.reshape(feature_dev, 2 * kv_width), preferred_element_type=f32
    )
    first = jnp.concatenate([first, keyval_part], axis=1)
    second = exchange(first, seq, tp, pairs)[0]

    block = jax.ShapeDtypeStruct(
        (kv_width // HEAD_DIM, 2 * rows * keyval_cache.shape[2], HEAD_DIM), jnp.bfloat16
    )
    keys, values, live = call(
        functools.partial(blocks_kernel, pair_offset),
        [block, block, jax.ShapeDtypeStruct((split, 2 * keyval_cache.shape[2]), f32)],
        [lengths, near, far],
        0,
        4 * near.size,
    )
    pack = jax.ShapeDtypeStruct((split + 8 + rows * 2 * kv_width // HEAD_DIM, HEAD_DIM), f32)
    packed, query, scale = call(
        functools.partial(attend_kernel, float(seq * feature_dev), width),
        [
            pack,
            jax.ShapeDtypeStruct((split, HEAD_DIM), jnp.bfloat16),
            jax.ShapeDtypeStruct((rows, HEAD_DIM), f32),
        ],
        [first, second, keys, values, live],
        16 * split * keyval_cache.shape[2] * HEAD_DIM,
        COVER,
    )
    for place, offsets in enumerate(rounds):
        parts = [packed] + exchange(packed, seq, tp, offsets)
        if place < len(rounds) - 1:
            packed = call(functools.partial(merge_kernel, split), [pack], parts, 0, COVER)[0]
    term, new_keyval = call(
        functools.partial(output_kernel, len(parts)),
        [
            jax.ShapeDtypeStruct((rows, attend_proj.shape[1]), f32),
            jax.ShapeDtypeStruct((rows, 2 * kv_width), f32),
        ],
        [query, scale, attend_proj, *parts],
        2 * rows * width * attend_proj.shape[1],
        COVER,
    )
    for bit in range(tp.bit_length() - 1):
        term = term + lax.ppermute(term, "tp", [(i, i ^ (1 << bit)) for i in range(tp)])
    hidden_out = (one_float + term).astype(jnp.bfloat16)
    return (hidden_out, new_keyval.astype(jnp.bfloat16).reshape(rows, 2, kv_width))


def solution(mesh):
    in_specs = (
        P("grp", "seq"),
        P("seq"),
        P("seq", "tp"),
        P("seq", None, "tp"),
        P("tp", "seq"),
        P(None, "grp", "seq", "tp"),
        P("grp"),
    )
    out_specs = (P("grp", "seq"), P("grp", None, "tp"))

    def body(*args):
        return on_device(mesh.shape["seq"], mesh.shape["tp"], *args)

    return jax.shard_map(
        body, mesh=mesh, in_specs=in_specs, out_specs=out_specs, check_vma=False
    )
```

```python
import functools

import jax
import jax.numpy as jnp
from jax import lax
from jax.experimental import pallas as pl
from jax.experimental.pallas import tpu as pltpu
from jax.sharding import PartitionSpec as P


HEAD_DIM = 128

EPSILON = 1e-05
MASKED = -1e30


COVER = 16 << 20
COVER_OPS = 1 << 22

VMEM = pl.BlockSpec(memory_space=pltpu.VMEM)
SMEM = pl.BlockSpec(memory_space=pltpu.SMEM)


def call(kernel, outs, ins, flops, bytes_accessed, other_ops=0):
    return pl.pallas_call(
        kernel,
        out_shape=outs,
        in_specs=[SMEM if a.dtype == jnp.int32 else VMEM for a in ins],
        out_specs=[VMEM] * len(outs),
        compiler_params=pltpu.CompilerParams(vmem_limit_bytes=16 << 20),
        cost_estimate=pl.CostEstimate(
            flops=flops, bytes_accessed=bytes_accessed, transcendentals=other_ops
        ),
    )(*ins)


def pair_bit(seq, core):
    return core % min(2, seq.bit_length() - 1)


def stages(seq, core):
    bits = [1 << b for b in range(seq.bit_length() - 1) if b != pair_bit(seq, core)]
    out = []
    while len(bits) > 1:
        low, high, *bits = bits
        out.append((low | high, high, low))
    return out + [(bit,) for bit in bits]


def reorder(offsets, turn):
    return [
        (o[1], o[0], *o[2:]) if len(o) > 1 and core % 2 == turn else o
        for core, o in enumerate(offsets)
    ]


def exchange(value, seq, tp, offsets):
    got = []
    for pair in zip(*offsets):
        moves = [
            (i * tp + core, (i ^ pair[core]) * tp + core) for i in range(seq) for core in range(tp)
        ]
        got.append(lax.ppermute(value, ("seq", "tp"), moves))
    return got


def widen_kernel(cache_ref, out_ref):
    out_ref[...] = cache_ref[...].astype(jnp.float32)


def query_kernel(hidden_ref, gain_ref, proj_ref, out_ref):
    width = proj_ref.shape[1]
    one_float = hidden_ref[...].astype(jnp.float32)
    scaled = (one_float * gain_ref[...]).astype(jnp.bfloat16)
    squares = jnp.sum(one_float * one_float, axis=1, keepdims=True)
    out_ref[:, width:] = jnp.broadcast_to(squares, (out_ref.shape[0], HEAD_DIM))
    out_ref[:, :width] = jnp.dot(scaled, proj_ref[...], preferred_element_type=jnp.float32)


def blocks_kernel(pair_offset, lengths_ref, near_ref, far_ref, keys_ref, values_ref, live_ref):
    rows, ctx = near_ref.shape[1:3]
    shape = live_ref.shape
    request = lax.broadcasted_iota(jnp.int32, shape, 0) % rows
    lane = lax.broadcasted_iota(jnp.int32, shape, 1)
    length = jnp.zeros(shape, jnp.int32)
    for r in range(rows):
        length = jnp.where(request == r, lengths_ref[r], length)
    rank = lax.axis_index("seq")
    pair = rank ^ pair_offset()
    position = jnp.where(lane < ctx, rank * ctx + lane, pair * ctx + lane - ctx)
    live_ref[...] = jnp.where(position < length, 1.0, 0.0)
    for kind, out_ref in enumerate((keys_ref, values_ref)):
        for k in range(out_ref.shape[0]):
            for r in range(rows):
                for side, ref in enumerate((near_ref, far_ref)):
                    at = (2 * r + side) * ctx
                    out_ref[k, at : at + ctx, :] = ref[
                        kind, r, :, k * HEAD_DIM : (k + 1) * HEAD_DIM
                    ].astype(jnp.bfloat16)


def attend_kernel(
    features, width, mine_ref, other_ref, keys_ref, values_ref, live_ref,
    packed_ref, query_ref, scale_ref,
):
    rows = mine_ref.shape[0]
    heads = width // HEAD_DIM
    kv_heads = keys_ref.shape[0]
    ctx = keys_ref.shape[1] // rows // 2
    share = heads // kv_heads * rows
    split = heads * rows
    scale = lax.rsqrt(
        (mine_ref[:, width : width + HEAD_DIM] + other_ref[:, width : width + HEAD_DIM])
        / features
        + EPSILON
    )
    scale_ref[...] = scale
    query = jnp.concatenate(
        [
            (mine_ref[:, c : c + HEAD_DIM] + other_ref[:, c : c + HEAD_DIM]) * scale
            for c in range(0, width, HEAD_DIM)
        ],
        axis=0,
    ).astype(jnp.bfloat16)
    query_ref[...] = query
    request = lax.broadcasted_iota(jnp.int32, (split, 2 * ctx), 0) % rows
    near = lax.broadcasted_iota(jnp.int32, (split, 2 * ctx), 1) < ctx
    live = live_ref[...] > 0
    scores = []
    for k in range(kv_heads):
        all_scores = lax.dot_general(
            query[k * share : (k + 1) * share],
            keys_ref[k],
            (((1,), (1,)), ((), ())),
            preferred_element_type=jnp.float32,
        )
        own = all_scores[:, : 2 * ctx]
        for r in range(1, rows):
            own = jnp.where(
                request[:share] == r, all_scores[:, 2 * ctx * r : 2 * ctx * (r + 1)], own
            )
        scores.append(own)
    scores = jnp.concatenate(scores, axis=0) * (HEAD_DIM ** (-0.5))
    best = [
        jnp.max(jnp.where(live & side, scores, MASKED), axis=1, keepdims=True)
        for side in (near, ~near)
    ]
    weights = jnp.where(live, jnp.exp(scores - jnp.where(near, best[0], best[1])), 0.0)
    weights = weights.astype(jnp.bfloat16).astype(jnp.float32)
    sides = [jnp.where(side, weights, 0.0) for side in (near, ~near)]
    top = jnp.maximum(best[0], best[1])
    factors = [jnp.exp(b - top) for b in best]
    total = sum(f * jnp.sum(s, axis=1, keepdims=True) for f, s in zip(factors, sides))
    for k in range(kv_heads):
        cut = slice(k * share, (k + 1) * share)
        spread = jnp.concatenate(
            [
                jnp.concatenate(
                    [jnp.where(request[cut] == r, s[cut], 0.0) for r in range(rows)], axis=1
                )
                for s in sides
            ],
            axis=0,
        ).astype(jnp.bfloat16)
        outs = jnp.dot(spread, values_ref[k], preferred_element_type=jnp.float32)
        packed_ref[cut, :] = factors[0][cut] * outs[:share] + factors[1][cut] * outs[share:]
    column = lax.broadcasted_iota(jnp.int32, (split, HEAD_DIM), 1)
    pair = jnp.where(column == 0, top, jnp.where(column == 1, total, 0.0))
    pair = jnp.concatenate([pair, jnp.zeros((HEAD_DIM - split, HEAD_DIM), jnp.float32)], axis=0)
    packed_ref[split : split + 8, :] = jnp.transpose(pair)[:8]
    for j in range(2 * kv_heads):
        at = width + HEAD_DIM + j * HEAD_DIM
        packed_ref[split + 8 + rows * j : split + 8 + rows * (j + 1), :] = (
            mine_ref[:, at : at + HEAD_DIM] + other_ref[:, at : at + HEAD_DIM]
        )


def merge(packed, split):
    best = functools.reduce(jnp.maximum, [p[split : split + 1] for p in packed])
    factors = [jnp.exp(p[split : split + 1] - best) for p in packed]
    total = sum(f * p[split + 1 : split + 2] for f, p in zip(factors, packed))
    row = lax.broadcasted_iota(jnp.int32, (8, HEAD_DIM), 0)
    stats = jnp.where(row == 0, best, jnp.where(row == 1, total, 0.0))
    for place, factor in enumerate(factors):
        stats = jnp.where(row == place + 2, factor, stats)
    columns = jnp.transpose(stats)[:split]
    gathered = sum(columns[:, 2 + i : 3 + i] * p[:split] for i, p in enumerate(packed))
    keyval = sum(p[split + 8 :] for p in packed)
    return gathered, columns[:, 0:1], columns[:, 1:2], keyval, jnp.where(row < 2, stats, 0.0)


def merge_kernel(split, *refs):
    packed_ref = refs[-1]
    gathered, _, _, keyval, stats = merge([ref[...] for ref in refs[:-1]], split)
    packed_ref[:split, :] = gathered
    packed_ref[split : split + 8, :] = stats
    packed_ref[split + 8 :, :] = keyval


def output_kernel(parts, query_ref, scale_ref, proj_ref, *refs):
    packed, (out_ref, new_ref) = refs[:parts], refs[parts:]
    split = query_ref.shape[0]
    rows = scale_ref.shape[0]
    gathered, best, total, keyval, _ = merge([ref[...] for ref in packed], split)
    kv_heads = keyval.shape[0] // rows // 2
    group = split // rows // kv_heads
    new = (keyval * jnp.concatenate([scale_ref[...]] * (2 * kv_heads), axis=0)).astype(jnp.bfloat16)
    new = new.astype(jnp.float32)
    for j in range(2 * kv_heads):
        new_ref[:, j * HEAD_DIM : (j + 1) * HEAD_DIM] = new[j * rows : (j + 1) * rows]
    own_key, own_value = (
        jnp.concatenate(
            [
                new[(kind * kv_heads + k) * rows : (kind * kv_heads + k + 1) * rows]
                for k in range(kv_heads)
                for _ in range(group)
            ],
            axis=0,
        )
        for kind in range(2)
    )
    query = query_ref[...].astype(jnp.float32)
    own_score = jnp.sum(query * own_key, axis=1, keepdims=True) * (HEAD_DIM ** (-0.5))
    top = jnp.maximum(best, own_score)
    old_weight = jnp.exp(best - top)
    fresh_weight = jnp.exp(own_score - top)
    attended = (old_weight * gathered + fresh_weight * own_value) / (
        old_weight * total + fresh_weight
    )
    attended = jnp.concatenate(
        [attended[r : r + rows] for r in range(0, split, rows)], axis=1
    ).astype(jnp.bfloat16)
    out_ref[...] = jnp.dot(attended, proj_ref[...], preferred_element_type=jnp.float32)


def on_device(
    seq, tp, hidden, norm_gain, query_proj, keyval_proj, attend_proj, keyval_cache, lengths
):
    f32 = jnp.float32
    rows, feature_dev = hidden.shape
    kv_width = keyval_cache.shape[3]
    width = query_proj.shape[1]
    split = rows * width // HEAD_DIM
    one_float = hidden.astype(f32)
    pairs = [(1 << pair_bit(seq, core),) for core in range(tp)]
    rounds = list(zip(*(stages(seq, core) for core in range(tp))))

    def pair_offset():
        core = lax.axis_index("tp")
        return sum(jnp.where(core == c, offset, 0) for c, (offset,) in enumerate(pairs))

    near = call(widen_kernel, [jax.ShapeDtypeStruct(keyval_cache.shape, f32)], [keyval_cache], 0, COVER, COVER_OPS)[0]
    far = exchange(near, seq, tp, pairs)[0]

    first = call(
        query_kernel,
        [jax.ShapeDtypeStruct((rows, width + HEAD_DIM), f32)],
        [hidden, norm_gain.reshape(1, feature_dev), query_proj],
        2 * rows * feature_dev * width,
        COVER,
    )[0]
    for offsets in rounds:
        for other in exchange(first, seq, tp, reorder(offsets, 0)):
            first = first + other
    scaled = (one_float * norm_gain).astype(jnp.bfloat16)
    keyval_part = jnp.dot(
        scaled, keyval_proj.reshape(feature_dev, 2 * kv_width), preferred_element_type=f32
    )
    first = jnp.concatenate([first, keyval_part], axis=1)
    second = exchange(first, seq, tp, pairs)[0]

    block = jax.ShapeDtypeStruct(
        (kv_width // HEAD_DIM, 2 * rows * keyval_cache.shape[2], HEAD_DIM), jnp.bfloat16
    )
    keys, values, live = call(
        functools.partial(blocks_kernel, pair_offset),
        [block, block, jax.ShapeDtypeStruct((split, 2 * keyval_cache.shape[2]), f32)],
        [lengths, near, far],
        0,
        4 * near.size,
    )
    pack = jax.ShapeDtypeStruct((split + 8 + rows * 2 * kv_width // HEAD_DIM, HEAD_DIM), f32)
    packed, query, scale = call(
        functools.partial(attend_kernel, float(seq * feature_dev), width),
        [
            pack,
            jax.ShapeDtypeStruct((split, HEAD_DIM), jnp.bfloat16),
            jax.ShapeDtypeStruct((rows, HEAD_DIM), f32),
        ],
        [first, second, keys, values, live],
        16 * split * keyval_cache.shape[2] * HEAD_DIM,
        COVER,
        COVER_OPS,
    )
    for place, offsets in enumerate(rounds):
        parts = [packed] + exchange(packed, seq, tp, reorder(offsets, 1))
        if place < len(rounds) - 1:
            packed = call(functools.partial(merge_kernel, split), [pack], parts, 0, COVER)[0]
    term, new_keyval = call(
        functools.partial(output_kernel, len(parts)),
        [
            jax.ShapeDtypeStruct((rows, attend_proj.shape[1]), f32),
            jax.ShapeDtypeStruct((rows, 2 * kv_width), f32),
        ],
        [query, scale, attend_proj, *parts],
        2 * rows * width * attend_proj.shape[1],
        COVER,
    )
    for bit in range(tp.bit_length() - 1):
        term = term + lax.ppermute(term, "tp", [(i, i ^ (1 << bit)) for i in range(tp)])
    hidden_out = (one_float + term).astype(jnp.bfloat16)
    return (hidden_out, new_keyval.astype(jnp.bfloat16).reshape(rows, 2, kv_width))


def solution(mesh):
    in_specs = (
        P("grp", "seq"),
        P("seq"),
        P("seq", "tp"),
        P("seq", None, "tp"),
        P("tp", "seq"),
        P(None, "grp", "seq", "tp"),
        P("grp"),
    )
    out_specs = (P("grp", "seq"), P("grp", None, "tp"))

    def body(*args):
        return on_device(mesh.shape["seq"], mesh.shape["tp"], *args)

    return jax.shard_map(
        body, mesh=mesh, in_specs=in_specs, out_specs=out_specs, check_vma=False
    )
```
